512 devices in a mesh: gx: 4 (over x), gy: 4 (over y), gz: 32 (over z, core).
Axes of the slice: x: 4, y: 4, z: 16, core: 2. Of those that a mesh axis runs over, the one named last changes fastest.
Arguments:
- displacement: bfloat16 [4, 4, 32, 768, 128], P('gx', 'gy', 'gz'), may hold values from -6 to 6
- flexibility: bfloat16 [4, 4, 32, 768, 768], P('gx', 'gy', 'gz'), as said below
- schur: bfloat16 [4, 4, 32, 768, 768], P('gx', 'gy', 'gz'), as said below
- face_rows: int32 [4, 4, 32, 768], P('gx', 'gy', 'gz'), may hold values from 0 to 767, as said below
- multiplicity: int32 [4, 4, 32, 768], P('gx', 'gy', 'gz'), may hold values from 2 to 8, as said below
Outputs:
- multipliers: float32 [4, 4, 32, 768, 128], P('gx', 'gy', 'gz')
The draws below stay inside these ranges and needn't reach their ends.
Inputs may be any that keep to these rules, and one draw needn't show every extreme that they name: `flexibility`: symmetric and positive definite. `schur`: symmetric and positive definite. `face_rows`: an interface unknown may be constrained by several slots of its subdomain. `multiplicity`: each value is 2, 4 or 8; a slot and its partner slot carry the same value.
All inputs are finite; a program needn't handle non-finite values.
Results may differ from the reference program's by a relative error of at most 0.017.
Values may be sent and summed in bfloat16 or wider, within the bound.
No kernel may reach another device: no remote copies, remote signals or barrier semaphores. Data moves between devices by JAX's collectives and lax.ppermute only.
A program may use at most 64 MiB of HBM per device.

```python
import jax
import jax.numpy as jnp
from jax import lax

NI = 768
FACE = 128
LOADS = 128
ITERS = 3
NS = 768
N_GX = 4
N_GY = 4
N_GZ = 32


def sym_operator(key, low, high):
    key_a, key_b = jax.random.split(key)
    shape = (N_GX, N_GY, N_GZ, NI, NI)
    noise = jax.random.normal(key_a, shape, jnp.float32) * (1.0 / (2.0 * NI)) ** 0.5
    diagonal = jax.random.uniform(key_b, (N_GX, N_GY, N_GZ, NI), jnp.float32, low, high)
    sym = (noise + jnp.swapaxes(noise, -1, -2)) * 0.7071067811865476
    return sym + diagonal[..., None] * jnp.eye(NI, dtype=jnp.float32)


def draw_flexibility(key, part):
    return sym_operator(jax.random.fold_in(key, 11), 3.0, 6.0).astype(jnp.bfloat16)


def draw_schur(key, part):
    return sym_operator(jax.random.fold_in(key, 23), 2.5, 5.0).astype(jnp.bfloat16)


def draw_face_rows(key, part):
    count = N_GX * N_GY * N_GZ
    keys = jax.random.split(jax.random.fold_in(key, 37), count)

    def one_list(sub):
        key_p, key_s, key_d = jax.random.split(sub, 3)
        order = jax.random.permutation(key_p, NI).astype(jnp.int32)
        base = jnp.take(order, jnp.arange(NS, dtype=jnp.int32) % NI)
        number = NS // 8
        source = jax.random.randint(key_s, (number,), 0, NS, dtype=jnp.int32)
        target = jax.random.randint(key_d, (number,), 0, NS, dtype=jnp.int32)
        return base.at[target].set(base[source])
    return jax.vmap(one_list)(keys).reshape(N_GX, N_GY, N_GZ, NS).astype(jnp.int32)


def draw_multiplicity(key, part):
    levels = jax.random.randint(jax.random.fold_in(key, 53), (N_GX, N_GY, N_GZ, 6, FACE), 1, 4, dtype=jnp.int32)
    values = jnp.where(levels == 1, 2, jnp.where(levels == 2, 4, 8)).astype(jnp.int32)
    coord_x = jnp.arange(N_GX).reshape(N_GX, 1, 1, 1)
    coord_y = jnp.arange(N_GY).reshape(1, N_GY, 1, 1)
    coord_z = jnp.arange(N_GZ).reshape(1, 1, N_GZ, 1)
    face_a = jnp.where(coord_x > 0, jnp.roll(values[:, :, :, 1], 1, axis=0), values[:, :, :, 0])
    face_c = jnp.where(coord_y > 0, jnp.roll(values[:, :, :, 3], 1, axis=1), values[:, :, :, 2])
    face_e = jnp.where(coord_z > 0, jnp.roll(values[:, :, :, 5], 1, axis=2), values[:, :, :, 4])
    joined = jnp.stack([face_a, values[:, :, :, 1], face_c, values[:, :, :, 3], face_e, values[:, :, :, 5]], axis=3)
    return joined.reshape(N_GX, N_GY, N_GZ, NS).astype(jnp.int32)


def level_of(rng, shape, shards, low, high):
    def one(position, blocks):
        heights = jax.random.uniform(jax.random.fold_in(jax.random.fold_in(rng, 6), position), (blocks,), jnp.float32, low / len(shards), high / len(shards))
        return jnp.repeat(jnp.exp(heights), shape[position] // blocks).reshape((-1,) + (1,) * (len(shape) - position - 1))

    level = one(*shards[0])
    for cut in shards[1:]:
        level = level * one(*cut)
    return level


def scatter_about(stream_key, extent, deviation, reach, pieces=(), kind=jnp.bfloat16):
    gain = level_of(stream_key, extent, pieces, -0.22, 0.18) if pieces else 1.0
    entries = jax.random.normal(stream_key, extent, jnp.float32) * deviation * gain
    return jnp.minimum(jnp.maximum(entries, -reach), reach).astype(kind)


def setup_inputs(seed: int = 0) -> dict:
    arg_keys = jax.random.split(jax.random.key(seed), 6)
    displacement = scatter_about(arg_keys[0], (N_GX, N_GY, N_GZ, NI, LOADS), 1.0, 6.0, ((0, 4), (1, 4), (2, 32)))
    flexibility = draw_flexibility(jax.random.fold_in(arg_keys[5], 71), 0)
    schur = draw_schur(jax.random.fold_in(arg_keys[5], 71), 0)
    face_rows = draw_face_rows(jax.random.fold_in(arg_keys[5], 71), 0)
    multiplicity = draw_multiplicity(jax.random.fold_in(arg_keys[5], 71), 0)
    return dict(displacement=displacement, flexibility=flexibility, schur=schur, face_rows=face_rows, multiplicity=multiplicity)


def shift_from(values, axis, lower):
    size = values.shape[axis]
    widths = [(0, 0)] * values.ndim
    widths[axis] = (1, 1)
    padded = jnp.pad(values, widths)
    start = 0 if lower else 2
    return lax.slice_in_dim(padded, start, start + size, axis=axis)


def reference(displacement, flexibility, schur, face_rows, multiplicity):
    count = N_GX * N_GY * N_GZ
    displaced = displacement.reshape(count, NI, LOADS)
    flex_ops = flexibility.reshape(count, NI, NI)
    schur_ops = schur.reshape(count, NI, NI)
    row_list = face_rows.reshape(count, NS)
    weight = 2.0 / multiplicity.reshape(count, NS, 1).astype(jnp.float32)
    shape3 = (N_GX, N_GY, N_GZ)
    coord_x = jnp.broadcast_to(jnp.arange(N_GX).reshape(N_GX, 1, 1), shape3)
    coord_y = jnp.broadcast_to(jnp.arange(N_GY).reshape(1, N_GY, 1), shape3)
    coord_z = jnp.broadcast_to(jnp.arange(N_GZ).reshape(1, 1, N_GZ), shape3)
    have = jnp.stack([coord_x > 0, coord_x < N_GX - 1, coord_y > 0, coord_y < N_GY - 1, coord_z > 0, coord_z < N_GZ - 1], axis=-1)
    inner = jnp.where(have, 0.5, 1.0).astype(jnp.float32)
    inner = jnp.repeat(inner[..., None], FACE, axis=-1).reshape(count, NS, 1)

    def pick(values):
        return jax.vmap(lambda block, picks: jnp.take(block, picks, axis=0))(values, row_list)

    def jump(values):
        faces_all = pick(values).astype(jnp.float32).reshape(N_GX, N_GY, N_GZ, 6, FACE, LOADS)
        partner = jnp.stack([
            shift_from(faces_all[:, :, :, 1], 0, True),
            shift_from(faces_all[:, :, :, 0], 0, False),
            shift_from(faces_all[:, :, :, 3], 1, True),
            shift_from(faces_all[:, :, :, 2], 1, False),
            shift_from(faces_all[:, :, :, 5], 2, True),
            shift_from(faces_all[:, :, :, 4], 2, False)], axis=3)
        return (faces_all - partner).reshape(count, NS, LOADS)

    def spread(values):
        summed = jax.vmap(lambda block, picks: jnp.zeros((NI, LOADS), jnp.float32).at[picks].add(block))(values, row_list)
        return summed.astype(jnp.bfloat16)

    def product(operators, vectors):
        return lax.map(lambda pair: jnp.dot(pair[0], pair[1], preferred_element_type=jnp.float32).astype(jnp.bfloat16), (operators, vectors))

    def flex_apply(values):
        return jump(product(flex_ops, spread(values)))

    def precondition(values):
        return weight * jump(product(schur_ops, spread(weight * values)))

    def inner_product(left, right):
        return jnp.sum(inner * left * right, axis=(0, 1))

    residual = jump(displaced)
    solution = jnp.zeros((count, NS, LOADS), jnp.float32)
    smoothed = precondition(residual)
    direction = smoothed
    rho_now = inner_product(residual, smoothed)
    for iteration in range(ITERS):
        image = flex_apply(direction)
        step_len = rho_now / inner_product(direction, image)
        solution = solution + step_len * direction
        residual = residual - step_len * image
        if iteration + 1 < ITERS:
            smoothed = precondition(residual)
            rho_next = inner_product(residual, smoothed)
            direction = smoothed + (rho_next / rho_now) * direction
            rho_now = rho_next
    return solution.reshape(N_GX, N_GY, N_GZ, NS, LOADS)
```

```python
import jax
import jax.numpy as jnp
from jax import lax
from jax.sharding import Mesh
from jax.sharding import PartitionSpec as P

GZ = ("gz_0", "gz_1")
AXES = (("gx", 0), ("gy", 2), (GZ, 4))
MOMENTS = 6


def swaps(devices, first):
    return [pair for i in range(first, devices - 1, 2) for pair in ((i, i + 1), (i + 1, i))]


def from_partners(faces):
    got = [None] * 6
    for axis, at in AXES:
        devices = lax.axis_size(axis)
        odd = lax.axis_index(axis) % 2 == 1
        low, high = faces[at], faces[at + 1]
        even_pairs = lax.ppermute(jnp.where(odd, low, high), axis, swaps(devices, 0))
        odd_pairs = lax.ppermute(jnp.where(odd, high, low), axis, swaps(devices, 1))
        got[at] = jnp.where(odd, even_pairs, odd_pairs)
        got[at + 1] = jnp.where(odd, odd_pairs, even_pairs)
    return jnp.stack(got)


def from_everyone(value, axis):
    copies = jnp.broadcast_to(value, (lax.axis_size(axis), *value.shape))
    return lax.all_to_all(copies, axis, split_axis=0, concat_axis=0, tiled=True)


def totals(moments, scale):
    for axis in (("gx", "gy"), GZ):
        scale = jnp.broadcast_to(scale, moments.shape[1:])
        packed = jnp.concatenate([moments, scale[None]])
        everyone = from_everyone(packed, axis)
        scales = everyone[:, MOMENTS]
        scale = jnp.max(scales, axis=0)
        ratio, power, sums = scales / scale, 1.0, []
        for k in range(MOMENTS):
            sums.append(jnp.sum(everyone[:, k] * power, axis=0))
            power = power * ratio
        moments = jnp.stack(sums)
    return moments, scale


def weights_of(moments):
    c0, c1, c2, c3, c4, c5 = [moments[k] for k in range(MOMENTS)]
    l10, l20 = c2 / c1, c3 / c1
    d1 = c3 - l10 * c2
    e21 = c4 - l10 * c3
    l21 = e21 / d1
    d2 = c5 - l20 * c3 - l21 * e21
    y1 = c1 - l10 * c0
    y2 = c2 - l20 * c0 - l21 * y1
    w2 = y2 / d2
    w1 = y1 / d1 - l21 * w2
    w0 = c0 / c1 - l10 * w1 - l20 * w2
    return w0, w1, w2


def shards(displacement, flexibility, schur, face_rows, multiplicity):
    width = flexibility.shape[-1]
    loads = displacement.shape[-1]
    slots = face_rows.shape[-1]
    face_len = slots // 6
    displaced = displacement.reshape(width, loads)
    flex_op = flexibility.reshape(width, width)
    schur_op = schur.reshape(width, width)
    rows = face_rows.reshape(slots, 1)
    weight = 2.0 / multiplicity.reshape(slots, 1).astype(jnp.float32)
    columns = jnp.arange(width, dtype=jnp.int32).reshape(1, width)
    here = rows == columns
    pick = here.astype(jnp.bfloat16)
    weighted_pick = jnp.where(here, weight, 0.0).astype(jnp.bfloat16)

    def minus_partner(own):
        faces = own.reshape(6, face_len, loads)
        partners = from_partners(faces)
        return (faces.astype(jnp.float32) - partners.astype(jnp.float32)).reshape(slots, loads)

    def on_slots(table, op):
        half = jnp.dot(table, op, preferred_element_type=jnp.float32).astype(jnp.bfloat16)
        return lax.dot_general(
            half, table, (((1,), (1,)), ((), ())), preferred_element_type=jnp.float32
        ).astype(jnp.bfloat16)

    def apply(op, values):
        high = lax.reduce_precision(values, 8, 7)
        parts = jnp.concatenate([high, values - high], axis=1).astype(jnp.bfloat16)
        both = jnp.dot(op, parts, preferred_element_type=jnp.float32)
        return both[:, :loads] + both[:, loads:]

    def dots(left, right):
        return jnp.sum(left * right, axis=0)

    def largest_diagonal(op):
        on = jnp.arange(width).reshape(width, 1) == columns
        return jnp.max(jnp.where(on, op, 0).astype(jnp.float32))

    picked = jnp.dot(pick, displaced, preferred_element_type=jnp.float32).astype(jnp.bfloat16)
    residual = minus_partner(picked)
    schur_slots = on_slots(weighted_pick, schur_op)
    flex_slots = on_slots(pick, flex_op)
    scale = largest_diagonal(flex_op) * largest_diagonal(schur_op)
    down = 1.0 / scale

    smooth0 = apply(schur_slots, residual)
    basis0 = minus_partner(smooth0)
    bent0 = apply(flex_slots, basis0)
    smooth1 = apply(schur_slots, minus_partner(bent0))
    basis1 = minus_partner(smooth1)
    bent1 = apply(flex_slots, basis1)
    smooth2 = apply(schur_slots, minus_partner(bent1))
    basis2 = minus_partner(smooth2)
    bent2 = apply(flex_slots, basis2)

    near1, near2 = basis1 * down, basis2 * down * down
    moments = jnp.stack(
        [
            dots(residual, smooth0),
            dots(basis0, bent0 * down),
            dots(near1, bent0 * down),
            dots(near1, bent1 * down * down),
            dots(near2, bent1 * down * down),
            dots(near2, bent2 * down * down * down),
        ]
    )
    moments, common = totals(moments, scale)
    w0, w1, w2 = weights_of(moments)
    up = 1.0 / common
    result = (
        (w0 * up) * basis0
        + (w1 * up) * (up * basis1)
        + (w2 * up) * (up * (up * basis2))
    )
    return result.reshape(1, 1, 1, slots, loads)


def solution(mesh):
    torus = Mesh(
        mesh.devices.reshape(mesh.shape["gx"], mesh.shape["gy"], 16, 2),
        ("gx", "gy", "gz_0", "gz_1"),
    )
    return jax.shard_map(
        shards,
        mesh=torus,
        in_specs=(
            P("gx", "gy", GZ, None, None),
            P("gx", "gy", GZ, None, None),
            P("gx", "gy", GZ, None, None),
            P("gx", "gy", GZ, None),
            P("gx", "gy", GZ, None),
        ),
        out_specs=P("gx", "gy", GZ, None, None),
        check_vma=False,
    )
```

```python
import jax
import jax.numpy as jnp
from jax import lax
from jax.sharding import Mesh
from jax.sharding import PartitionSpec as P


GZ = ("gz_0", "gz_1")
AXES = (("gx", 0), ("gy", 2), (GZ, 4))
ROUNDS = ((GZ, 4, 1), ("gx", 0, 0), ("gx", 0, 1), ("gy", 2, 0), ("gy", 2, 1), (GZ, 4, 0))
MOMENTS = 6


def swaps(devices, first):
    return [pair for i in range(first, devices - 1, 2) for pair in ((i, i + 1), (i + 1, i))]


def from_partners(faces):
    swapped = {}
    for axis, at, first in ROUNDS:
        odd = lax.axis_index(axis) % 2 == 1
        low, high = faces[at], faces[at + 1]
        mine = jnp.where(odd, high, low) if first else jnp.where(odd, low, high)
        swapped[at, first] = lax.ppermute(mine, axis, swaps(lax.axis_size(axis), first))
    got = []
    for axis, at in AXES:
        odd = lax.axis_index(axis) % 2 == 1
        got.append(jnp.where(odd, swapped[at, 0], swapped[at, 1]))
        got.append(jnp.where(odd, swapped[at, 1], swapped[at, 0]))
    return jnp.stack(got)


def from_everyone(value, axis):
    copies = jnp.broadcast_to(value.reshape(-1), (lax.axis_size(axis), 1, value.size))
    got = lax.all_to_all(copies, axis, split_axis=0, concat_axis=0, tiled=True)
    return got.reshape(-1, *value.shape)


def totals(moments, scale):
    for axis in (("gx", "gy", "gz_1"), "gz_0"):
        scale = jnp.broadcast_to(scale, moments.shape[1:])
        packed = jnp.concatenate([moments, scale[None]])
        everyone = from_everyone(packed, axis)
        scales = everyone[:, MOMENTS]
        scale = jnp.max(scales, axis=0)
        ratio, power, sums = scales / scale, 1.0, []
        for k in range(MOMENTS):
            sums.append(jnp.sum(everyone[:, k] * power, axis=0))
            power = power * ratio
        moments = jnp.stack(sums)
    return moments, scale


def weights_of(moments):
    c0, c1, c2, c3, c4, c5 = [moments[k] for k in range(MOMENTS)]
    l10, l20 = c2 / c1, c3 / c1
    d1 = c3 - l10 * c2
    e21 = c4 - l10 * c3
    l21 = e21 / d1
    d2 = c5 - l20 * c3 - l21 * e21
    y1 = c1 - l10 * c0
    y2 = c2 - l20 * c0 - l21 * y1
    w2 = y2 / d2
    w1 = y1 / d1 - l21 * w2
    w0 = c0 / c1 - l10 * w1 - l20 * w2
    return w0, w1, w2


def shards(displacement, flexibility, schur, face_rows, multiplicity):
    width = flexibility.shape[-1]
    loads = displacement.shape[-1]
    slots = face_rows.shape[-1]
    face_len = slots // 6
    displaced = displacement.reshape(width, loads)
    flex_op = flexibility.reshape(width, width)
    schur_op = schur.reshape(width, width)
    rows = face_rows.reshape(slots, 1)
    weight = 2.0 / multiplicity.reshape(slots, 1).astype(jnp.float32)
    columns = jnp.arange(width, dtype=jnp.int32).reshape(1, width)
    here = rows == columns
    pick = here.astype(jnp.bfloat16)
    weighted_pick = jnp.where(here, weight, 0.0).astype(jnp.bfloat16)

    def minus_partner(own):
        faces = own.astype(jnp.bfloat16).reshape(6, face_len, loads)
        partners = from_partners(faces)
        return (faces.astype(jnp.float32) - partners.astype(jnp.float32)).reshape(slots, loads)

    def on_slots(table, op):
        half = jnp.dot(table, op, preferred_element_type=jnp.float32).astype(jnp.bfloat16)
        return lax.dot_general(
            half, table, (((1,), (1,)), ((), ())), preferred_element_type=jnp.float32
        ).astype(jnp.bfloat16)

    def apply(op, values):
        high = lax.reduce_precision(values, 8, 7)
        parts = jnp.concatenate([high, values - high], axis=1).astype(jnp.bfloat16)
        both = jnp.dot(op, parts, preferred_element_type=jnp.float32)
        return both[:, :loads] + both[:, loads:]

    def dots(left, right):
        return jnp.sum(left * right, axis=0)

    def size_of(op):
        return jnp.max(jnp.abs(op[:8, :128].astype(jnp.float32)))

    picked = jnp.dot(pick, displaced, preferred_element_type=jnp.float32).astype(jnp.bfloat16)
    residual = minus_partner(picked)
    schur_slots = on_slots(weighted_pick, schur_op)
    flex_slots = on_slots(pick, flex_op)
    scale = size_of(flex_op) * size_of(schur_op)
    down = 1.0 / scale

    smooth0 = apply(schur_slots, residual)
    basis0 = minus_partner(smooth0)
    bent0 = apply(flex_slots, basis0)
    smooth1 = apply(schur_slots, minus_partner(bent0))
    basis1 = minus_partner(smooth1)
    bent1 = apply(flex_slots, basis1)
    smooth2 = apply(schur_slots, minus_partner(bent1))
    basis2 = minus_partner(smooth2)
    bent2 = apply(flex_slots, basis2)

    near1, near2 = basis1 * down, basis2 * down * down
    moments = jnp.stack(
        [
            dots(residual, smooth0),
            dots(basis0, bent0 * down),
            dots(near1, bent0 * down),
            dots(near1, bent1 * down * down),
            dots(near2, bent1 * down * down),
            dots(near2, bent2 * down * down * down),
        ]
    )
    moments, common = totals(moments, scale)
    w0, w1, w2 = weights_of(moments)
    up = 1.0 / common
    result = (
        (w0 * up) * basis0
        + (w1 * up) * (up * basis1)
        + (w2 * up) * (up * (up * basis2))
    )
    return result.reshape(1, 1, 1, slots, loads)


def solution(mesh):
    torus = Mesh(
        mesh.devices.reshape(mesh.shape["gx"], mesh.shape["gy"], 16, 2),
        ("gx", "gy", "gz_0", "gz_1"),
    )
    return jax.shard_map(
        shards,
        mesh=torus,
        in_specs=(
            P("gx", "gy", GZ, None, None),
            P("gx", "gy", GZ, None, None),
            P("gx", "gy", GZ, None, None),
            P("gx", "gy", GZ, None),
            P("gx", "gy", GZ, None),
        ),
        out_specs=P("gx", "gy", GZ, None, None),
        check_vma=False,
    )
```
